1024 devices in a mesh: row: 64 (over x, y), col: 16 (over z, core).
Axes of the slice: x: 8, y: 8, z: 8, core: 2. Of those that a mesh axis runs over, the one named last changes fastest.
Arguments:
- matrix: float32 [32768, 8192], P('row', 'col'), may hold values from -50 to 50, as said below
Outputs:
- updated: float32 [32768, 8192], P('row', 'col')
- coefficients: float32 [512, 8192], P(None, 'col')
The draws below stay inside these ranges and needn't reach their ends.
Inputs may be any that keep to these rules, and one draw needn't show every extreme that they name: `matrix`: real values of order one to some tens.
All inputs are finite; a program needn't handle non-finite values.
Results may differ from the reference program's by a relative error of at most 0.00014.
Values sent between devices are 32-bit elements; how exact they have to be, the bound alone decides.
A program may use at most 64 MiB of HBM per device.

```python
import math
import jax
import jax.numpy as jnp
from jax import lax

PANEL = 256
COL_DEV = 512
ROWS = 32768
COLS = 8192


def draw_matrix(key, part):
    keys = jax.random.split(jax.random.fold_in(key, 7), 3)
    ramp = jnp.arange(ROWS, dtype=jnp.float32) / ROWS
    row_scales = jnp.exp(ramp * math.log(3.0) + jax.random.uniform(keys[1], (ROWS,), jnp.float32, 0.0, math.log(3.4))) / 3.0
    col_scales = jnp.exp(jax.random.uniform(keys[2], (COLS,), jnp.float32, 0.0, math.log(10.0))) / math.sqrt(10.0)
    entries = jnp.clip(jax.random.normal(keys[0], (ROWS, COLS), jnp.float32), -4.0, 4.0)
    return entries * row_scales[:, None] * col_scales[None, :]


def setup_inputs(seed: int = 0) -> dict:
    arg_keys = jax.random.split(jax.random.key(seed), 2)
    matrix = draw_matrix(jax.random.fold_in(arg_keys[1], 71), 0)
    return {"matrix": matrix}


def reference(matrix):
    stretch = math.sqrt(ROWS)
    current = matrix
    collected = []
    for panel_no in range(2):
        start = panel_no * COL_DEV
        panel_cols = current[:, start:start + PANEL]
        gram_matrix = jnp.dot(panel_cols.T, panel_cols, precision=lax.Precision.HIGHEST)
        triangle = jnp.linalg.cholesky(gram_matrix)
        basis_t = lax.linalg.triangular_solve(triangle, panel_cols.T, left_side=True, lower=True)
        weights = jnp.dot(basis_t, current, precision=lax.Precision.HIGHEST)
        current = current - jnp.dot(basis_t.T, weights, precision=lax.Precision.HIGHEST)
        current = current.at[:, start:start + PANEL].set(stretch * basis_t.T)
        collected.append(weights)
    return (current, jnp.concatenate(collected, axis=0))
```

```python
import functools
import math

import jax
import jax.numpy as jnp
from jax import lax
from jax.experimental import pallas as pl
from jax.experimental.pallas import tpu as pltpu
from jax.sharding import PartitionSpec as P

PANEL = 256
N = 8
CH = 8
CR = PANEL // CH
PIECE = 64
SUBS = ((0, 40), (40, 32))
MESH = pl.DeviceIdType.MESH
HI = lax.Precision.HIGHEST
F32 = jnp.float32


def wrap(i):
    return lax.rem(i + 2 * N, N)


def tdot(a, b, precision=HI):
    return lax.dot_general(a, b, (((0,), (0,)), ((), ())), precision=precision, preferred_element_type=F32)


def dot(a, b, precision=HI):
    return lax.dot_general(a, b, (((1,), (0,)), ((), ())), precision=precision, preferred_element_type=F32)


def dott(a, b, precision=HI):
    return lax.dot_general(a, b, (((1,), (1,)), ((), ())), precision=precision, preferred_element_type=F32)


def reduce_kernel(
    x_ref, p_ref, cf, gall,
    own, rf, rb, stage, r2, gtmp,
    zs, zr, cs, cr,
    fs, fr, bs, br,
    s2, q2, s3, q3, sg, qg,
    afs, afr, abs_, abr,
    gfs, gfr, gbs, gbr, gcs, gcr,
):
    row, col = lax.axis_index("row"), lax.axis_index("col")
    xx, yy = row // N, lax.rem(row, N)
    zz, cc = col // 2, lax.rem(col, 2)
    fwd = 1 - 2 * cc
    main, other = (xx, yy), (yy, xx)

    def at_main(k, m):
        return (m * N + yy, col) if k == 0 else (xx * N + m, col)

    def at_other(k, o):
        return at_main(1 - k, o)

    def at_z(z):
        return (row, wrap(z) * 2 + cc)

    mate = (row, zz * 2 + 1 - cc)

    def remote(src, dst, send, recv, device):
        return pltpu.make_async_remote_copy(
            src_ref=src, dst_ref=dst, send_sem=send, recv_sem=recv, device_id=device, device_id_type=MESH
        )

    barrier = pltpu.get_barrier_semaphore()
    partners = [at_main(k, wrap(main[k] + o)) for k in range(2) for o in range(1, N)]
    partners += [at_z(zz + 1), at_z(zz - 1), mate]
    for device in partners:
        pl.semaphore_signal(barrier, inc=1, device_id=device, device_id_type=MESH)
    pl.semaphore_wait(barrier, len(partners))

    def chunk(h, i):
        return pl.ds(pl.multiple_of(h * PANEL + i * CR, CR), CR)

    def z_copy(h, i, src):
        target = p_ref.at[cc, chunk(h, i), :]
        return remote(src, target, zs.at[h, i], zr.at[h, i], at_z(zz + 1 - 2 * h))

    def mate_copy(h, i, src):
        target = p_ref.at[cc, chunk(h, i), :]
        return remote(src, target, cs.at[h, i], cr.at[h, i], mate)

    @pl.when(zz == 0)
    def _():
        @pl.loop(0, CH)
        def _(i):
            for h in range(2):
                z_copy(h, i, x_ref.at[chunk(h, i), pl.ds(0, PANEL)]).start()
            for h in range(2):
                mate_copy(h, i, x_ref.at[chunk(h, i), pl.ds(0, PANEL)]).start()

        p_ref[cc] = x_ref[:, :PANEL]

    @pl.when(zz != 0)
    def _():
        @pl.loop(0, CH)
        def _(i):
            for h in range(2):
                here = p_ref.at[cc, chunk(h, i), :]
                z_copy(h, i, here).wait_recv()

                @pl.when(zz != (N - 1 if h == 0 else 1))
                def _():
                    z_copy(h, i, here).start()

                mate_copy(h, i, here).start()

    @pl.loop(0, CH)
    def _(i):
        for h in range(2):
            pltpu.make_async_remote_copy(
                src_ref=p_ref.at[1 - cc, chunk(h, i), :],
                dst_ref=p_ref.at[1 - cc, chunk(h, i), :],
                send_sem=cs.at[h, i],
                recv_sem=cr.at[h, i],
                device_id=mate,
                device_id_type=MESH,
            ).wait_recv()

    x = x_ref[...]

    @pl.loop(0, 4)
    def _(b):
        block = p_ref[b // 2, :, pl.ds(pl.multiple_of(128 * lax.rem(b, 2), 128), 128)]
        terms = tdot(block, x)
        for k in range(2):
            for j in range(2):
                own[k, 2 * b + j, 0:PIECE, :] = terms[PIECE * j : PIECE * (j + 1), PANEL * k : PANEL * (k + 1)]

    gb = col // 4
    block = p_ref[gb // 2, :, pl.ds(pl.multiple_of(128 * lax.rem(gb, 2), 128), 128)]
    for k in range(2):
        gtmp[k] = tdot(block, p_ref[k])
    for k in range(2):
        for j in range(N):
            first = pl.multiple_of(32 * lax.rem(col, 4) + 8 * (j // 2), 8)
            own[k, j, PIECE : PIECE + 8, 0:128] = gtmp[k, pl.ds(first, 8), 128 * (j % 2) : 128 * (j % 2) + 128]
            own[k, j, PIECE : PIECE + 8, 128:PANEL] = jnp.zeros((8, PANEL - 128), F32)

    def f_copy(k, s, u):
        rows = pl.ds(*SUBS[u])
        src = own.at[k, wrap(main[k] + 4 * fwd), rows, :] if s == 0 else rf.at[k, s - 1, rows, :]
        return remote(src, rf.at[k, s, rows, :], fs.at[k, s, u], fr.at[k, s, u], at_main(k, wrap(main[k] + fwd)))

    def b_copy(k, s, u):
        rows = pl.ds(*SUBS[u])
        src = own.at[k, wrap(main[k] - 3 * fwd), rows, :] if s == 0 else rb.at[k, s - 1, rows, :]
        return remote(src, rb.at[k, s, rows, :], bs.at[k, s, u], br.at[k, s, u], at_main(k, wrap(main[k] - fwd)))

    for u in range(2):
        for k in range(2):
            f_copy(k, 0, u).start()
            b_copy(k, 0, u).start()
    for s in range(1, 4):
        for u in range(2):
            rows = pl.ds(*SUBS[u])
            for k in range(2):
                f_copy(k, s - 1, u).wait_recv()
                rf[k, s - 1, rows, :] += own[k, wrap(main[k] + (4 - s) * fwd), rows, :]
                f_copy(k, s, u).start()
                if s < 3:
                    b_copy(k, s - 1, u).wait_recv()
                    rb[k, s - 1, rows, :] += own[k, wrap(main[k] - (3 - s) * fwd), rows, :]
                    b_copy(k, s, u).start()
    for k in range(2):
        for u in range(2):
            b_copy(k, 2, u).wait_recv()
            f_copy(k, 3, u).wait_recv()
        total = own[k, main[k]] + rf[k, 3] + rb[k, 2]
        for i in range(N):
            stage[k, i, 0:8, :] = total[8 * i : 8 * i + 8, :]
            stage[k, i, 8:16, :] = total[PIECE : PIECE + 8, :]
        for o in range(1, N):
            peer = wrap(other[k] + o)
            remote(stage.at[k, peer], r2.at[k, other[k]], s2.at[k, o - 1], q2.at[k, other[k]], at_other(k, peer)).start()
        r2[k, other[k]] = stage[k, other[k]]

    def mine(k):
        return pl.ds(pl.multiple_of(PIECE * main[k] + 8 * other[k], 8), 8)

    for k in range(2):
        for o in range(1, N):
            peer = wrap(other[k] + o)
            remote(stage.at[k, peer], r2.at[k, peer], s2.at[k, o - 1], q2.at[k, peer], at_other(k, peer)).wait_recv()
        total = r2[k, 0]
        for o in range(1, N):
            total = total + r2[k, o]
        cf[k, mine(k), :] = total[0:8, :]
        gall[col, k, main[k]] = total[8:16, 0:128]
        for o in range(1, N):
            peer = wrap(main[k] + o)
            tile = gall.at[col, k, main[k]]
            remote(tile, tile, sg.at[k, o - 1], qg.at[k, main[k]], at_main(k, peer)).start()
        for o in range(1, N):
            peer = wrap(other[k] + o)
            rows = cf.at[k, mine(k), :]
            remote(rows, rows, s3.at[k, o - 1], q3.at[k, other[k]], at_other(k, peer)).start()

    def gf_copy(s):
        slab = gall.at[wrap(zz - s * fwd) * 2 + cc]
        return remote(slab, slab, gfs.at[s], gfr.at[s], at_z(zz + fwd))

    def gb_copy(s):
        slab = gall.at[wrap(zz + s * fwd) * 2 + cc]
        return remote(slab, slab, gbs.at[s], gbr.at[s], at_z(zz - fwd))

    def gf_wait(s):
        slab = gall.at[wrap(zz - (s + 1) * fwd) * 2 + cc]
        remote(slab, slab, gfs.at[s], gfr.at[s], at_z(zz + fwd)).wait_recv()

    def gb_wait(s):
        slab = gall.at[wrap(zz + (s + 1) * fwd) * 2 + cc]
        remote(slab, slab, gbs.at[s], gbr.at[s], at_z(zz - fwd)).wait_recv()

    def g_mate(z):
        slab = gall.at[z * 2 + cc]
        return remote(slab, slab, gcs.at[z], gcr.at[z], mate)

    for k in range(2):
        for o in range(1, N):
            peer = wrap(main[k] + o)
            tile = gall.at[col, k, peer]
            remote(tile, tile, sg.at[k, o - 1], qg.at[k, peer], at_main(k, peer)).wait_recv()
    gf_copy(0).start()
    gb_copy(0).start()
    g_mate(zz).start()

    def piece(k, m, u):
        return cf.at[k, pl.ds(pl.multiple_of(PIECE * wrap(m) + 32 * u, 32), 32), :]

    def af_copy(k, s, u, m):
        return remote(piece(k, m, u), piece(k, m, u), afs.at[k, s, u], afr.at[k, s, u], at_main(k, wrap(main[k] + fwd)))

    def ab_copy(k, s, u, m):
        return remote(piece(k, m, u), piece(k, m, u), abs_.at[k, s, u], abr.at[k, s, u], at_main(k, wrap(main[k] - fwd)))

    for k in range(2):
        for o in range(1, N):
            peer = wrap(other[k] + o)
            rows = cf.at[k, pl.ds(pl.multiple_of(PIECE * main[k] + 8 * peer, 8), 8), :]
            remote(rows, rows, s3.at[k, o - 1], q3.at[k, peer], at_other(k, peer)).wait_recv()
        for u in range(2):
            af_copy(k, 0, u, main[k]).start()
            ab_copy(k, 0, u, main[k]).start()
    for s in range(1, 5):
        for u in range(2):
            for k in range(2):
                af_copy(k, s - 1, u, main[k] - s * fwd).wait_recv()
                if s < 4:
                    af_copy(k, s, u, main[k] - s * fwd).start()
                    ab_copy(k, s - 1, u, main[k] + s * fwd).wait_recv()
                if s < 3:
                    ab_copy(k, s, u, main[k] + s * fwd).start()
        gf_wait(s - 1)
        if s < 4:
            gf_copy(s).start()
        g_mate(wrap(zz - s * fwd)).start()
        if s < 4:
            gb_wait(s - 1)
            if s < 3:
                gb_copy(s).start()
            g_mate(wrap(zz + s * fwd)).start()
    for z in range(N):
        slab = gall.at[z * 2 + 1 - cc]
        remote(slab, slab, gcs.at[z], gcr.at[z], mate).wait_recv()

    @pl.loop(0, CH)
    def _(i):
        for h in range(2):
            here = p_ref.at[cc, chunk(h, i), :]
            mate_copy(h, i, here).wait_send()

            @pl.when(zz != (N - 1 if h == 0 else 1))
            def _():
                z_copy(h, i, here).wait_send()

    for k in range(2):
        for u in range(2):
            for s in range(4):
                f_copy(k, s, u).wait_send()
                af_copy(k, s, u, main[k]).wait_send()
            for s in range(3):
                b_copy(k, s, u).wait_send()
                ab_copy(k, s, u, main[k]).wait_send()
        for o in range(1, N):
            peer = wrap(other[k] + o)
            remote(stage.at[k, peer], r2.at[k, peer], s2.at[k, o - 1], q2.at[k, peer], at_other(k, peer)).wait_send()
            rows = cf.at[k, mine(k), :]
            remote(rows, rows, s3.at[k, o - 1], q3.at[k, peer], at_other(k, peer)).wait_send()
            tile = gall.at[col, k, main[k]]
            remote(tile, tile, sg.at[k, o - 1], qg.at[k, peer], at_main(k, wrap(main[k] + o))).wait_send()
    for s in range(4):
        gf_copy(s).wait_send()
    for s in range(3):
        gb_copy(s).wait_send()
    for z in range(N):
        g_mate(z).wait_send()


def reduced(matrix):
    dma = pltpu.SemaphoreType.DMA
    out = lambda *shape: jax.ShapeDtypeStruct(shape, F32)
    vmem = pl.BlockSpec(memory_space=pltpu.VMEM)
    return pl.pallas_call(
        reduce_kernel,
        out_shape=(out(2, 512, PANEL), out(2, 512, PANEL), out(16, 2, N, 8, 128)),
        in_specs=[vmem],
        out_specs=(vmem, vmem, vmem),
        scratch_shapes=[
            pltpu.VMEM((2, N, 72, PANEL), F32),
            pltpu.VMEM((2, 4, 72, PANEL), F32),
            pltpu.VMEM((2, 3, 72, PANEL), F32),
            pltpu.VMEM((2, N, 16, PANEL), F32),
            pltpu.VMEM((2, N, 16, PANEL), F32),
            pltpu.VMEM((2, 128, PANEL), F32),
            dma((2, CH)), dma((2, CH)), dma((2, CH)), dma((2, CH)),
            dma((2, 4, 2)), dma((2, 4, 2)), dma((2, 3, 2)), dma((2, 3, 2)),
            dma((2, N - 1)), dma((2, N)), dma((2, N - 1)), dma((2, N)), dma((2, N - 1)), dma((2, N)),
            dma((2, 4, 2)), dma((2, 4, 2)), dma((2, 3, 2)), dma((2, 3, 2)),
            dma((4,)), dma((4,)), dma((3,)), dma((3,)), dma((N,)), dma((N,)),
        ],
        compiler_params=pltpu.CompilerParams(collective_id=0, has_side_effects=True),
    )(matrix)


def solve_kernel(stretch, x_ref, p_ref, cf, gall, upd, w_ref, g, m, t, e, bt, dcol, drow):
    n = 2 * PANEL
    col = lax.axis_index("col")

    @pl.loop(0, 16)
    def _(c):
        for k in range(2):
            for j in range(N):
                rows = pl.ds(pl.multiple_of(32 * c + 8 * (j // 2), 8), 8)
                g[rows, PANEL * k + 128 * (j % 2) : PANEL * k + 128 * (j % 2) + 128] = gall[c, k, j]

    i_row = lax.broadcasted_iota(jnp.int32, (n, n), 0)
    i_col = lax.broadcasted_iota(jnp.int32, (n, n), 1)
    eye = i_row == i_col
    diagonal = jnp.where(eye, g[...], 0.0)
    dcol[...] = lax.rsqrt(jnp.sum(diagonal, axis=1, keepdims=True))
    drow[...] = lax.rsqrt(jnp.sum(diagonal, axis=0, keepdims=True))
    g[...] = g[...] * dcol[...] * drow[...]

    def half_lower(v):
        return jnp.where(i_row > i_col, v, jnp.where(eye, 0.5 * v, 0.0))

    ident = jnp.where(eye, 1.0, 0.0)
    m[...] = ident - half_lower(g[...] - ident)

    halves = [pl.ds(0, PANEL), pl.ds(PANEL, PANEL)]

    def refine(precision):
        for h in halves:
            t[:, h] = dot(m[...], g[:, h], precision)
        for h in halves:
            e[:, h] = dott(t[...], m[h, :], precision)
        e[...] = e[...] - ident
        square = jnp.sum(e[...] * e[...])
        e[...] = half_lower(e[...])
        for h in halves:
            t[:, h] = m[:, h] - dot(e[...], m[:, h], precision)
        m[...] = t[...]
        return square

    refine(HI)
    refine(HI)
    left = refine(HI)

    @pl.when(jnp.logical_not(left < 1e-6))
    def _():
        t[...] = ident

        @pl.loop(0, n)
        def _(j):
            g_row = g[pl.ds(j, 1), :]
            t_row = t[pl.ds(j, 1), :]
            lane = lax.broadcasted_iota(jnp.int32, (n, n), 1)
            column = jnp.sum(jnp.where(lane == j, g[...], 0.0), axis=1, keepdims=True)
            one_lane = lax.broadcasted_iota(jnp.int32, (1, n), 1)
            pivot = jnp.sum(jnp.where(one_lane == j, g_row, 0.0), axis=1, keepdims=True)
            down = lax.broadcasted_iota(jnp.int32, (n, 1), 0)
            factor = jnp.where(down > j, column / pivot, 0.0)
            scale = jnp.where(down == j, lax.rsqrt(pivot), 1.0)
            g[...] = g[...] - factor * g_row
            t[...] = (t[...] - factor * t_row) * scale

        m[...] = t[...]

    m[...] = m[...] * drow[...]
    top, low = halves
    w_top = w_ref.at[top, :]
    for k, h in enumerate(halves):
        c_top, c_low = cf[k, top, :], cf[k, low, :]
        w_ref[top, h] = dot(m[top, top], c_top)
        w_ref[low, h] = dot(m[low, top], c_top) + dot(m[low, low], c_low)
    bt[:, top] = dott(p_ref[0], m[top, top])
    bt[:, low] = dott(p_ref[0], m[low, top]) + dott(p_ref[1], m[low, low])
    upd[:, low] = x_ref[:, low] - dot(bt[...], w_ref[:, low])
    first = x_ref[:, top] - dot(bt[:, top], w_ref[top, top])
    first = jnp.where(col == 0, stretch * bt[:, top], first)
    first = first - dot(bt[:, low], w_ref[low, top])
    upd[:, top] = jnp.where(col == 1, stretch * bt[:, low], first)


def solved(stretch, matrix, panels, cross, gram):
    vmem = pl.BlockSpec(memory_space=pltpu.VMEM)
    square = pltpu.VMEM((512, 512), F32)
    return pl.pallas_call(
        functools.partial(solve_kernel, stretch),
        out_shape=(jax.ShapeDtypeStruct((512, 512), F32), jax.ShapeDtypeStruct((512, 512), F32)),
        in_specs=[vmem] * 4,
        out_specs=(vmem, vmem),
        scratch_shapes=[square] * 5 + [pltpu.VMEM((512, 1), F32), pltpu.VMEM((1, 512), F32)],
    )(matrix, panels, cross, gram)


def body(matrix):
    stretch = math.sqrt(lax.axis_size("row") * matrix.shape[0])
    panels, cross, gram = reduced(matrix)
    return solved(stretch, matrix, panels, cross, gram)


def solution(mesh):
    in_specs = (P("row", "col"),)
    out_specs = (P("row", "col"), P(None, "col"))
    return jax.shard_map(body, mesh=mesh, in_specs=in_specs, out_specs=out_specs, check_vma=False)
```

```python
import functools
import math

import jax
import jax.numpy as jnp
from jax import lax
from jax.experimental import pallas as pl
from jax.experimental.pallas import tpu as pltpu
from jax.sharding import PartitionSpec as P

PANEL = 256
N = 8
CH = 16
CR = 512 // CH
PIECE = 64
PEERS = (1, N - 1, 2, N - 2, 3, N - 3, 4)
MESH = pl.DeviceIdType.MESH
HI = lax.Precision.HIGHEST
F32 = jnp.float32


def wrap(i):
    return lax.rem(i + 2 * N, N)


def tdot(a, b, precision=HI):
    return lax.dot_general(a, b, (((0,), (0,)), ((), ())), precision=precision, preferred_element_type=F32)


def dot(a, b, precision=HI):
    return lax.dot_general(a, b, (((1,), (0,)), ((), ())), precision=precision, preferred_element_type=F32)


def dott(a, b, precision=HI):
    return lax.dot_general(a, b, (((1,), (1,)), ((), ())), precision=precision, preferred_element_type=F32)


def reduce_kernel(
    x_ref, p_ref, cf, gall,
    own, r1, stage, r2, gtmp,
    zs, zr, cs, cr,
    s1, q1, s2, q2, s3, q3, s4, q4,
    sg, qg, sz, qz, sc, qc,
):
    row, col = lax.axis_index("row"), lax.axis_index("col")
    xx, yy = row // N, lax.rem(row, N)
    zz, cc = col // 2, lax.rem(col, 2)
    step = 1 - 2 * (zz // 5)
    main, other = (xx, yy), (yy, xx)

    def at_main(k, m):
        return (m * N + yy, col) if k == 0 else (xx * N + m, col)

    def at_other(k, o):
        return at_main(1 - k, o)

    def at_z(z):
        return (row, wrap(z) * 2 + cc)

    mate = (row, zz * 2 + 1 - cc)

    def remote(src, dst, send, recv, device):
        return pltpu.make_async_remote_copy(
            src_ref=src, dst_ref=dst, send_sem=send, recv_sem=recv, device_id=device, device_id_type=MESH
        )

    barrier = pltpu.get_barrier_semaphore()
    partners = [at_main(k, wrap(main[k] + o)) for k in range(2) for o in range(1, N)]
    partners += [at_z(zz + o) for o in range(1, N)] + [mate]
    for device in partners:
        pl.semaphore_signal(barrier, inc=1, device_id=device, device_id_type=MESH)
    pl.semaphore_wait(barrier, len(partners))

    def chunk(i):
        return pl.ds(pl.multiple_of(i * CR, CR), CR)

    def z_copy(h, i, src, z):
        return remote(src, p_ref.at[cc, chunk(i), :], zs.at[h, i], zr.at[i], at_z(z))

    def mate_copy(i, src):
        return remote(src, p_ref.at[cc, chunk(i), :], cs.at[i], cr.at[i], mate)

    @pl.when(zz == 0)
    def _():
        @pl.loop(0, CH)
        def _(i):
            here = x_ref.at[chunk(i), pl.ds(0, PANEL)]
            z_copy(0, i, here, 1).start()
            z_copy(1, i, here, N - 1).start()
            mate_copy(i, here).start()

        p_ref[cc] = x_ref[:, :PANEL]

    relays = (zz != 0) & (zz != 4) & (zz != 5)

    @pl.when(zz != 0)
    def _():
        @pl.loop(0, CH)
        def _(i):
            here = p_ref.at[cc, chunk(i), :]
            z_copy(0, i, here, zz + step).wait_recv()

            @pl.when(relays)
            def _():
                z_copy(0, i, here, zz + step).start()

            mate_copy(i, here).start()

    @pl.loop(0, CH)
    def _(i):
        here = p_ref.at[1 - cc, chunk(i), :]
        remote(here, here, cs.at[i], cr.at[i], mate).wait_recv()

    x = x_ref[...]

    @pl.loop(0, 4)
    def _(b):
        block = p_ref[b // 2, :, pl.ds(pl.multiple_of(128 * lax.rem(b, 2), 128), 128)]
        terms = tdot(block, x)
        for k in range(2):
            for j in range(2):
                own[k, 2 * b + j, 0:PIECE, :] = terms[PIECE * j : PIECE * (j + 1), PANEL * k : PANEL * (k + 1)]

    gb = col // 4
    block = p_ref[gb // 2, :, pl.ds(pl.multiple_of(128 * lax.rem(gb, 2), 128), 128)]
    for k in range(2):
        gtmp[k] = tdot(block, p_ref[k])
    for k in range(2):
        for j in range(N):
            first = pl.multiple_of(32 * lax.rem(col, 4) + 8 * (j // 2), 8)
            own[k, j, PIECE : PIECE + 8, 0:128] = gtmp[k, pl.ds(first, 8), 128 * (j % 2) : 128 * (j % 2) + 128]
            own[k, j, PIECE : PIECE + 8, 128:PANEL] = jnp.zeros((8, PANEL - 128), F32)

    def copy1(k, o, slot):
        peer = wrap(main[k] + o)
        return remote(own.at[k, peer], r1.at[k, slot], s1.at[k, o - 1], q1.at[k, slot], at_main(k, peer))

    def copy2(k, o, slot):
        peer = wrap(other[k] + o)
        return remote(stage.at[k, peer], r2.at[k, slot], s2.at[k, o - 1], q2.at[k, slot], at_other(k, peer))

    for o in PEERS:
        for k in range(2):
            copy1(k, o, main[k]).start()
    for k in range(2):
        r1[k, main[k]] = own[k, main[k]]
        for o in PEERS:
            copy1(k, o, wrap(main[k] + o)).wait_recv()
        total = r1[k, 0]
        for o in range(1, N):
            total = total + r1[k, o]
        for i in range(N):
            stage[k, i, 0:8, :] = total[8 * i : 8 * i + 8, :]
            stage[k, i, 8:16, :] = total[PIECE : PIECE + 8, :]
        for o in PEERS:
            copy2(k, o, other[k]).start()
        r2[k, other[k]] = stage[k, other[k]]

    def rows_of(k, i):
        return cf.at[k, pl.ds(pl.multiple_of(PIECE * main[k] + 8 * i, 8), 8), :]

    def piece_of(k, i):
        return cf.at[k, pl.ds(pl.multiple_of(PIECE * i, PIECE), PIECE), :]

    def copy3(k, o, i):
        return remote(rows_of(k, i), rows_of(k, i), s3.at[k, o - 1], q3.at[k, i], at_other(k, wrap(other[k] + o)))

    def copy4(k, o, i):
        return remote(piece_of(k, i), piece_of(k, i), s4.at[k, o - 1], q4.at[k, i], at_main(k, wrap(main[k] + o)))

    def tile_copy(k, o, i):
        tile = gall.at[col, k, i]
        return remote(tile, tile, sg.at[k, o - 1], qg.at[k, i], at_main(k, wrap(main[k] + o)))

    def slab_copy(o, z):
        slab = gall.at[z * 2 + cc]
        return remote(slab, slab, sz.at[o - 1], qz.at[z], at_z(zz + o))

    def slab_mate(z, core):
        slab = gall.at[z * 2 + core]
        return remote(slab, slab, sc.at[z], qc.at[z], mate)

    for k in range(2):
        for o in PEERS:
            copy2(k, o, wrap(other[k] + o)).wait_recv()
        total = r2[k, 0]
        for o in range(1, N):
            total = total + r2[k, o]
        gall[col, k, main[k]] = total[8:16, 0:128]
        cf[k, pl.ds(pl.multiple_of(PIECE * main[k] + 8 * other[k], 8), 8), :] = total[0:8, :]
        for o in PEERS:
            tile_copy(k, o, main[k]).start()
        for o in PEERS:
            copy3(k, o, other[k]).start()

    for k in range(2):
        for o in PEERS:
            tile_copy(k, o, wrap(main[k] + o)).wait_recv()
    for o in PEERS:
        slab_copy(o, zz).start()
    slab_mate(zz, cc).start()

    for k in range(2):
        for o in PEERS:
            copy3(k, o, wrap(other[k] + o)).wait_recv()
        for o in PEERS:
            copy4(k, o, main[k]).start()
    for o in PEERS:
        z = wrap(zz - o)
        slab_copy(o, z).wait_recv()
        slab_mate(z, cc).start()
    for k in range(2):
        for o in PEERS:
            copy4(k, o, wrap(main[k] + o)).wait_recv()
    for z in range(N):
        slab_mate(z, 1 - cc).wait_recv()

    @pl.loop(0, CH)
    def _(i):
        here = p_ref.at[cc, chunk(i), :]
        mate_copy(i, here).wait_send()

        @pl.when(relays | (zz == 0))
        def _():
            z_copy(0, i, here, zz + step).wait_send()

        @pl.when(zz == 0)
        def _():
            z_copy(1, i, here, N - 1).wait_send()

    for o in range(1, N):
        for k in range(2):
            copy1(k, o, main[k]).wait_send()
            copy2(k, o, other[k]).wait_send()
            copy3(k, o, other[k]).wait_send()
            copy4(k, o, main[k]).wait_send()
            tile_copy(k, o, main[k]).wait_send()
        slab_copy(o, zz).wait_send()
    for z in range(N):
        slab_mate(z, cc).wait_send()


def reduced(matrix):
    dma = pltpu.SemaphoreType.DMA
    out = lambda *shape: jax.ShapeDtypeStruct(shape, F32)
    vmem = pl.BlockSpec(memory_space=pltpu.VMEM)
    return pl.pallas_call(
        reduce_kernel,
        out_shape=(out(2, 512, PANEL), out(2, 512, PANEL), out(16, 2, N, 8, 128)),
        in_specs=[vmem],
        out_specs=(vmem, vmem, vmem),
        scratch_shapes=[
            pltpu.VMEM((2, N, 72, PANEL), F32),
            pltpu.VMEM((2, N, 72, PANEL), F32),
            pltpu.VMEM((2, N, 16, PANEL), F32),
            pltpu.VMEM((2, N, 16, PANEL), F32),
            pltpu.VMEM((2, 128, PANEL), F32),
            dma((2, CH)), dma((CH,)), dma((CH,)), dma((CH,)),
            *[dma((2, N))] * 8,
            dma((2, N)), dma((2, N)), dma((N,)), dma((N,)), dma((N,)), dma((N,)),
        ],
        compiler_params=pltpu.CompilerParams(collective_id=0, has_side_effects=True),
    )(matrix)


def solve_kernel(stretch, x_ref, p_ref, cf, gall, upd, w_ref, g, m, t, e, bt, dcol, drow):
    n = 2 * PANEL
    col = lax.axis_index("col")

    @pl.loop(0, 16)
    def _(c):
        for k in range(2):
            for j in range(N):
                rows = pl.ds(pl.multiple_of(32 * c + 8 * (j // 2), 8), 8)
                g[rows, PANEL * k + 128 * (j % 2) : PANEL * k + 128 * (j % 2) + 128] = gall[c, k, j]

    i_row = lax.broadcasted_iota(jnp.int32, (n, n), 0)
    i_col = lax.broadcasted_iota(jnp.int32, (n, n), 1)
    eye = i_row == i_col
    diagonal = jnp.where(eye, g[...], 0.0)
    dcol[...] = lax.rsqrt(jnp.sum(diagonal, axis=1, keepdims=True))
    drow[...] = lax.rsqrt(jnp.sum(diagonal, axis=0, keepdims=True))
    g[...] = g[...] * dcol[...] * drow[...]

    def half_lower(v):
        return jnp.where(i_row > i_col, v, jnp.where(eye, 0.5 * v, 0.0))

    ident = jnp.where(eye, 1.0, 0.0)
    m[...] = ident - half_lower(g[...] - ident)

    halves = [pl.ds(0, PANEL), pl.ds(PANEL, PANEL)]

    def refine(precision):
        for h in halves:
            t[:, h] = dot(m[...], g[:, h], precision)
        for h in halves:
            e[:, h] = dott(t[...], m[h, :], precision)
        e[...] = e[...] - ident
        square = jnp.sum(e[...] * e[...])
        e[...] = half_lower(e[...])
        for h in halves:
            t[:, h] = m[:, h] - dot(e[...], m[:, h], precision)
        m[...] = t[...]
        return square

    refine(HI)
    refine(HI)
    left = refine(HI)

    @pl.when(jnp.logical_not(left < 1e-6))
    def _():
        t[...] = ident

        @pl.loop(0, n)
        def _(j):
            g_row = g[pl.ds(j, 1), :]
            t_row = t[pl.ds(j, 1), :]
            lane = lax.broadcasted_iota(jnp.int32, (n, n), 1)
            column = jnp.sum(jnp.where(lane == j, g[...], 0.0), axis=1, keepdims=True)
            one_lane = lax.broadcasted_iota(jnp.int32, (1, n), 1)
            pivot = jnp.sum(jnp.where(one_lane == j, g_row, 0.0), axis=1, keepdims=True)
            down = lax.broadcasted_iota(jnp.int32, (n, 1), 0)
            factor = jnp.where(down > j, column / pivot, 0.0)
            scale = jnp.where(down == j, lax.rsqrt(pivot), 1.0)
            g[...] = g[...] - factor * g_row
            t[...] = (t[...] - factor * t_row) * scale

        m[...] = t[...]

    m[...] = m[...] * drow[...]
    top, low = halves
    for k, h in enumerate(halves):
        c_top, c_low = cf[k, top, :], cf[k, low, :]
        w_ref[top, h] = dot(m[top, top], c_top)
        w_ref[low, h] = dot(m[low, top], c_top) + dot(m[low, low], c_low)
    bt[:, top] = dott(p_ref[0], m[top, top])
    bt[:, low] = dott(p_ref[0], m[low, top]) + dott(p_ref[1], m[low, low])
    upd[:, low] = x_ref[:, low] - dot(bt[...], w_ref[:, low])
    first = x_ref[:, top] - dot(bt[:, top], w_ref[top, top])
    first = jnp.where(col == 0, stretch * bt[:, top], first)
    first = first - dot(bt[:, low], w_ref[low, top])
    upd[:, top] = jnp.where(col == 1, stretch * bt[:, low], first)


def solved(stretch, matrix, panels, cross, gram):
    vmem = pl.BlockSpec(memory_space=pltpu.VMEM)
    square = pltpu.VMEM((512, 512), F32)
    return pl.pallas_call(
        functools.partial(solve_kernel, stretch),
        out_shape=(jax.ShapeDtypeStruct((512, 512), F32), jax.ShapeDtypeStruct((512, 512), F32)),
        in_specs=[vmem] * 4,
        out_specs=(vmem, vmem),
        scratch_shapes=[square] * 5 + [pltpu.VMEM((512, 1), F32), pltpu.VMEM((1, 512), F32)],
    )(matrix, panels, cross, gram)


def body(matrix):
    stretch = math.sqrt(lax.axis_size("row") * matrix.shape[0])
    panels, cross, gram = reduced(matrix)
    return solved(stretch, matrix, panels, cross, gram)


def solution(mesh):
    in_specs = (P("row", "col"),)
    out_specs = (P("row", "col"), P(None, "col"))
    return jax.shard_map(body, mesh=mesh, in_specs=in_specs, out_specs=out_specs, check_vma=False)
```

```python
import functools
import math

import jax
import jax.numpy as jnp
from jax import lax
from jax.experimental import pallas as pl
from jax.experimental.pallas import tpu as pltpu
from jax.sharding import PartitionSpec as P

PANEL = 256
N = 8
CH = 16
CR = 512 // CH
PIECE = 64
PEERS = (1, N - 1, 2, N - 2, 3, N - 3, 4)
MESH = pl.DeviceIdType.MESH
HI = lax.Precision.HIGHEST
F32 = jnp.float32


def wrap(i):
    return lax.rem(i + 2 * N, N)


def tdot(a, b, precision=HI):
    return lax.dot_general(a, b, (((0,), (0,)), ((), ())), precision=precision, preferred_element_type=F32)


def dot(a, b, precision=HI):
    return lax.dot_general(a, b, (((1,), (0,)), ((), ())), precision=precision, preferred_element_type=F32)


def dott(a, b, precision=HI):
    return lax.dot_general(a, b, (((1,), (1,)), ((), ())), precision=precision, preferred_element_type=F32)


def reduce_kernel(
    x_ref, p_ref, cf, gall,
    own, r1, stage, r2, gtmp,
    zs, zr, cs, cr,
    s1, q1, s2, q2, s3, q3, s4, q4,
    sg, qg, sz, qz, sc, qc,
):
    row, col = lax.axis_index("row"), lax.axis_index("col")
    xx, yy = row // N, lax.rem(row, N)
    zz, cc = col // 2, lax.rem(col, 2)
    step = 1 - 2 * (zz // 5)
    main, other = (xx, yy), (yy, xx)

    def at_main(k, m):
        return (m * N + yy, col) if k == 0 else (xx * N + m, col)

    def at_other(k, o):
        return at_main(1 - k, o)

    def at_z(z):
        return (row, wrap(z) * 2 + cc)

    mate = (row, zz * 2 + 1 - cc)

    def remote(src, dst, send, recv, device):
        return pltpu.make_async_remote_copy(
            src_ref=src, dst_ref=dst, send_sem=send, recv_sem=recv, device_id=device, device_id_type=MESH
        )

    barrier = pltpu.get_barrier_semaphore()
    partners = [at_main(k, wrap(main[k] + o)) for k in range(2) for o in range(1, N)]
    partners += [at_z(zz + o) for o in range(1, N)] + [mate]
    for device in partners:
        pl.semaphore_signal(barrier, inc=1, device_id=device, device_id_type=MESH)
    pl.semaphore_wait(barrier, len(partners))

    def chunk(i):
        return pl.ds(pl.multiple_of(i * CR, CR), CR)

    def z_copy(h, i, src, z):
        return remote(src, p_ref.at[cc, chunk(i), :], zs.at[h, i], zr.at[i], at_z(z))

    def mate_copy(i, src):
        return remote(src, p_ref.at[cc, chunk(i), :], cs.at[i], cr.at[i], mate)

    @pl.when(zz == 0)
    def _():
        @pl.loop(0, CH)
        def _(i):
            here = x_ref.at[chunk(i), pl.ds(0, PANEL)]
            z_copy(0, i, here, 1).start()
            z_copy(1, i, here, N - 1).start()
            mate_copy(i, here).start()

        p_ref[cc] = x_ref[:, :PANEL]

    relays = (zz != 0) & (zz != 4) & (zz != 5)

    @pl.when(zz != 0)
    def _():
        @pl.loop(0, CH)
        def _(i):
            here = p_ref.at[cc, chunk(i), :]
            z_copy(0, i, here, zz + step).wait_recv()

            @pl.when(relays)
            def _():
                z_copy(0, i, here, zz + step).start()

            mate_copy(i, here).start()

    @pl.loop(0, CH)
    def _(i):
        here = p_ref.at[1 - cc, chunk(i), :]
        remote(here, here, cs.at[i], cr.at[i], mate).wait_recv()

    x = x_ref[...]

    @pl.loop(0, 4)
    def _(b):
        block = p_ref[b // 2, :, pl.ds(pl.multiple_of(128 * lax.rem(b, 2), 128), 128)]
        terms = tdot(block, x)
        for k in range(2):
            for j in range(2):
                own[k, 2 * b + j, 0:PIECE, :] = terms[PIECE * j : PIECE * (j + 1), PANEL * k : PANEL * (k + 1)]

    gb = col // 4
    block = p_ref[gb // 2, :, pl.ds(pl.multiple_of(128 * lax.rem(gb, 2), 128), 128)]
    for k in range(2):
        gtmp[k] = tdot(block, p_ref[k])
    for k in range(2):
        for j in range(N):
            first = pl.multiple_of(32 * lax.rem(col, 4) + 8 * (j // 2), 8)
            own[k, j, PIECE : PIECE + 8, 0:128] = gtmp[k, pl.ds(first, 8), 128 * (j % 2) : 128 * (j % 2) + 128]
            own[k, j, PIECE : PIECE + 8, 128:PANEL] = jnp.zeros((8, PANEL - 128), F32)

    def copy1(k, o, slot):
        peer = wrap(main[k] + o)
        return remote(own.at[k, peer], r1.at[k, slot], s1.at[k, o - 1], q1.at[k, slot], at_main(k, peer))

    def copy2(k, o, slot):
        peer = wrap(other[k] + o)
        return remote(stage.at[k, peer], r2.at[k, slot], s2.at[k, o - 1], q2.at[k, slot], at_other(k, peer))

    for o in PEERS:
        for k in range(2):
            copy1(k, o, main[k]).start()
    for k in range(2):
        r1[k, main[k]] = own[k, main[k]]
        for o in PEERS:
            copy1(k, o, wrap(main[k] + o)).wait_recv()
        total = r1[k, 0]
        for o in range(1, N):
            total = total + r1[k, o]
        for i in range(N):
            stage[k, i, 0:8, :] = total[8 * i : 8 * i + 8, :]
            stage[k, i, 8:16, :] = total[PIECE : PIECE + 8, :]
        for o in PEERS:
            copy2(k, o, other[k]).start()
        r2[k, other[k]] = stage[k, other[k]]

    def rows_of(k, i):
        return cf.at[k, pl.ds(pl.multiple_of(PIECE * main[k] + 8 * i, 8), 8), :]

    def piece_of(k, i):
        return cf.at[k, pl.ds(pl.multiple_of(PIECE * i, PIECE), PIECE), :]

    def copy3(k, o, i):
        return remote(rows_of(k, i), rows_of(k, i), s3.at[k, o - 1], q3.at[k, i], at_other(k, wrap(other[k] + o)))

    def copy4(k, o, i):
        return remote(piece_of(k, i), piece_of(k, i), s4.at[k, o - 1], q4.at[k, i], at_main(k, wrap(main[k] + o)))

    def tile_copy(k, o, i):
        tile = gall.at[col, k, i]
        return remote(tile, tile, sg.at[k, o - 1], qg.at[k, i], at_main(k, wrap(main[k] + o)))

    def slab_copy(o, z):
        slab = gall.at[z * 2 + cc]
        return remote(slab, slab, sz.at[o - 1], qz.at[z], at_z(zz + o))

    def slab_mate(z, core):
        slab = gall.at[z * 2 + core]
        return remote(slab, slab, sc.at[z], qc.at[z], mate)

    for k in range(2):
        for o in PEERS:
            copy2(k, o, wrap(other[k] + o)).wait_recv()
        total = r2[k, 0]
        for o in range(1, N):
            total = total + r2[k, o]
        gall[col, k, main[k]] = total[8:16, 0:128]
        cf[k, pl.ds(pl.multiple_of(PIECE * main[k] + 8 * other[k], 8), 8), :] = total[0:8, :]
        for o in PEERS:
            tile_copy(k, o, main[k]).start()
        for o in PEERS:
            copy3(k, o, other[k]).start()

    for k in range(2):
        for o in PEERS:
            tile_copy(k, o, wrap(main[k] + o)).wait_recv()
    for o in PEERS:
        slab_copy(o, zz).start()
    slab_mate(zz, cc).start()

    for k in range(2):
        for o in PEERS:
            copy3(k, o, wrap(other[k] + o)).wait_recv()
        for o in PEERS:
            copy4(k, o, main[k]).start()
    for o in PEERS:
        z = wrap(zz - o)
        slab_copy(o, z).wait_recv()
        slab_mate(z, cc).start()
    for k in range(2):
        for o in PEERS:
            copy4(k, o, wrap(main[k] + o)).wait_recv()
    for z in range(N):
        slab_mate(z, 1 - cc).wait_recv()

    @pl.loop(0, CH)
    def _(i):
        here = p_ref.at[cc, chunk(i), :]
        mate_copy(i, here).wait_send()

        @pl.when(relays | (zz == 0))
        def _():
            z_copy(0, i, here, zz + step).wait_send()

        @pl.when(zz == 0)
        def _():
            z_copy(1, i, here, N - 1).wait_send()

    for o in range(1, N):
        for k in range(2):
            copy1(k, o, main[k]).wait_send()
            copy2(k, o, other[k]).wait_send()
            copy3(k, o, other[k]).wait_send()
            copy4(k, o, main[k]).wait_send()
            tile_copy(k, o, main[k]).wait_send()
        slab_copy(o, zz).wait_send()
    for z in range(N):
        slab_mate(z, cc).wait_send()


def reduced(matrix):
    dma = pltpu.SemaphoreType.DMA
    out = lambda *shape: jax.ShapeDtypeStruct(shape, F32)
    vmem = pl.BlockSpec(memory_space=pltpu.VMEM)
    return pl.pallas_call(
        reduce_kernel,
        out_shape=(out(2, 512, PANEL), out(2, 512, PANEL), out(16, 2, N, 8, 128)),
        in_specs=[vmem],
        out_specs=(vmem, vmem, vmem),
        scratch_shapes=[
            pltpu.VMEM((2, N, 72, PANEL), F32),
            pltpu.VMEM((2, N, 72, PANEL), F32),
            pltpu.VMEM((2, N, 16, PANEL), F32),
            pltpu.VMEM((2, N, 16, PANEL), F32),
            pltpu.VMEM((2, 128, PANEL), F32),
            dma((2, CH)), dma((CH,)), dma((CH,)), dma((CH,)),
            *[dma((2, N))] * 8,
            dma((2, N)), dma((2, N)), dma((N,)), dma((N,)), dma((N,)), dma((N,)),
        ],
        compiler_params=pltpu.CompilerParams(collective_id=0, has_side_effects=True),
    )(matrix)


def solve_kernel(stretch, x_ref, p_ref, cf, gall, upd, w_ref, g, m, t, e, bt, dcol, drow):
    n = 2 * PANEL
    col = lax.axis_index("col")

    @pl.loop(0, 16)
    def _(c):
        for k in range(2):
            for j in range(N):
                rows = pl.ds(pl.multiple_of(32 * c + 8 * (j // 2), 8), 8)
                g[rows, PANEL * k + 128 * (j % 2) : PANEL * k + 128 * (j % 2) + 128] = gall[c, k, j]

    i_row = lax.broadcasted_iota(jnp.int32, (n, n), 0)
    i_col = lax.broadcasted_iota(jnp.int32, (n, n), 1)
    eye = i_row == i_col
    diagonal = jnp.where(eye, g[...], 0.0)
    dcol[...] = lax.rsqrt(jnp.sum(diagonal, axis=1, keepdims=True))
    drow[...] = lax.rsqrt(jnp.sum(diagonal, axis=0, keepdims=True))
    g[...] = g[...] * dcol[...] * drow[...]

    ident = jnp.where(eye, 1.0, 0.0)
    b_row = lax.broadcasted_iota(jnp.int32, (PANEL, PANEL), 0)
    b_col = lax.broadcasted_iota(jnp.int32, (PANEL, PANEL), 1)
    b_eye = jnp.where(b_row == b_col, 1.0, 0.0)

    def half_lower(v):
        return jnp.where(b_row > b_col, v, 0.5 * b_eye * v)

    halves = [pl.ds(0, PANEL), pl.ds(PANEL, PANEL)]
    top, low = halves
    m[top, top] = b_eye - half_lower(g[top, top] - b_eye)
    m[low, low] = b_eye - half_lower(g[low, low] - b_eye)
    m[low, top] = -g[low, top]
    m[top, low] = jnp.zeros((PANEL, PANEL), F32)

    def refine(precision):
        t[top, top] = dot(m[top, top], g[top, top], precision)
        for h in halves:
            t[low, h] = dot(m[low, top], g[top, h], precision) + dot(m[low, low], g[low, h], precision)
        e00 = dott(t[top, top], m[top, top], precision) - b_eye
        e10 = dott(t[low, top], m[top, top], precision)
        e11 = dott(t[low, top], m[low, top], precision) + dott(t[low, low], m[low, low], precision) - b_eye
        square = jnp.sum(e00 * e00 + 2.0 * e10 * e10 + e11 * e11)
        e[top, top] = half_lower(e00)
        e[low, top] = e10
        e[low, low] = half_lower(e11)
        below = dot(e[low, top], m[top, top], precision) + dot(e[low, low], m[low, top], precision)
        m[low, top] = m[low, top] - below
        m[top, top] = m[top, top] - dot(e[top, top], m[top, top], precision)
        m[low, low] = m[low, low] - dot(e[low, low], m[low, low], precision)
        return square

    refine(lax.Precision.DEFAULT)
    refine(lax.Precision.HIGH)
    left = refine(HI)

    @pl.when(jnp.logical_not(left < 1e-6))
    def _():
        t[...] = ident

        @pl.loop(0, n)
        def _(j):
            g_row = g[pl.ds(j, 1), :]
            t_row = t[pl.ds(j, 1), :]
            lane = lax.broadcasted_iota(jnp.int32, (n, n), 1)
            column = jnp.sum(jnp.where(lane == j, g[...], 0.0), axis=1, keepdims=True)
            one_lane = lax.broadcasted_iota(jnp.int32, (1, n), 1)
            pivot = jnp.sum(jnp.where(one_lane == j, g_row, 0.0), axis=1, keepdims=True)
            down = lax.broadcasted_iota(jnp.int32, (n, 1), 0)
            factor = jnp.where(down > j, column / pivot, 0.0)
            scale = jnp.where(down == j, lax.rsqrt(pivot), 1.0)
            g[...] = g[...] - factor * g_row
            t[...] = (t[...] - factor * t_row) * scale

        m[...] = t[...]

    m[...] = m[...] * drow[...]
    for k, h in enumerate(halves):
        c_top, c_low = cf[k, top, :], cf[k, low, :]
        w_ref[top, h] = dot(m[top, top], c_top)
        w_ref[low, h] = dot(m[low, top], c_top) + dot(m[low, low], c_low)
    bt[:, top] = dott(p_ref[0], m[top, top])
    bt[:, low] = dott(p_ref[0], m[low, top]) + dott(p_ref[1], m[low, low])
    upd[:, low] = x_ref[:, low] - dot(bt[...], w_ref[:, low])
    first = x_ref[:, top] - dot(bt[:, top], w_ref[top, top])
    first = jnp.where(col == 0, stretch * bt[:, top], first)
    first = first - dot(bt[:, low], w_ref[low, top])
    upd[:, top] = jnp.where(col == 1, stretch * bt[:, low], first)


def solved(stretch, matrix, panels, cross, gram):
    vmem = pl.BlockSpec(memory_space=pltpu.VMEM)
    square = pltpu.VMEM((512, 512), F32)
    return pl.pallas_call(
        functools.partial(solve_kernel, stretch),
        out_shape=(jax.ShapeDtypeStruct((512, 512), F32), jax.ShapeDtypeStruct((512, 512), F32)),
        in_specs=[vmem] * 4,
        out_specs=(vmem, vmem),
        scratch_shapes=[square] * 5 + [pltpu.VMEM((512, 1), F32), pltpu.VMEM((1, 512), F32)],
    )(matrix, panels, cross, gram)


def body(matrix):
    stretch = math.sqrt(lax.axis_size("row") * matrix.shape[0])
    panels, cross, gram = reduced(matrix)
    return solved(stretch, matrix, panels, cross, gram)


def solution(mesh):
    in_specs = (P("row", "col"),)
    out_specs = (P("row", "col"), P(None, "col"))
    return jax.shard_map(body, mesh=mesh, in_specs=in_specs, out_specs=out_specs, check_vma=False)
```

```python
import functools
import math

import jax
import jax.numpy as jnp
from jax import lax
from jax.experimental import pallas as pl
from jax.experimental.pallas import tpu as pltpu
from jax.sharding import PartitionSpec as P

PANEL = 256
N = 8
CH = 16
CR = 512 // CH
PIECE = 64
PEERS = (1, N - 1, 2, N - 2, 3, N - 3, 4)
MESH = pl.DeviceIdType.MESH
HI = lax.Precision.HIGHEST
F32 = jnp.float32


def wrap(i):
    return lax.rem(i + 2 * N, N)


def tdot(a, b, precision=HI):
    return lax.dot_general(a, b, (((0,), (0,)), ((), ())), precision=precision, preferred_element_type=F32)


def dot(a, b, precision=HI):
    return lax.dot_general(a, b, (((1,), (0,)), ((), ())), precision=precision, preferred_element_type=F32)


def dott(a, b, precision=HI):
    return lax.dot_general(a, b, (((1,), (1,)), ((), ())), precision=precision, preferred_element_type=F32)


def reduce_kernel(
    x_ref, p_ref, cf, gall,
    own, r1, stage, r2, gtmp,
    zs, zr, cs, cr,
    s1, q1, s2, q2, s3, q3, s4, q4,
    sg, qg, sz, qz, sc, qc,
):
    row, col = lax.axis_index("row"), lax.axis_index("col")
    xx, yy = row // N, lax.rem(row, N)
    zz, cc = col // 2, lax.rem(col, 2)
    step = 1 - 2 * (zz // 5)
    main, other = (xx, yy), (yy, xx)

    def at_main(k, m):
        return (m * N + yy, col) if k == 0 else (xx * N + m, col)

    def at_other(k, o):
        return at_main(1 - k, o)

    def at_z(z):
        return (row, wrap(z) * 2 + cc)

    mate = (row, zz * 2 + 1 - cc)

    def remote(src, dst, send, recv, device):
        return pltpu.make_async_remote_copy(
            src_ref=src, dst_ref=dst, send_sem=send, recv_sem=recv, device_id=device, device_id_type=MESH
        )

    barrier = pltpu.get_barrier_semaphore()
    partners = [at_main(k, wrap(main[k] + o)) for k in range(2) for o in range(1, N)]
    partners += [at_z(zz + o) for o in range(1, N)] + [mate]
    for device in partners:
        pl.semaphore_signal(barrier, inc=1, device_id=device, device_id_type=MESH)
    pl.semaphore_wait(barrier, len(partners))

    def chunk(i):
        return pl.ds(pl.multiple_of(i * CR, CR), CR)

    def z_copy(h, i, src, z):
        return remote(src, p_ref.at[cc, chunk(i), :], zs.at[h, i], zr.at[i], at_z(z))

    def mate_copy(i, src):
        return remote(src, p_ref.at[cc, chunk(i), :], cs.at[i], cr.at[i], mate)

    @pl.when(zz == 0)
    def _():
        @pl.loop(0, CH)
        def _(i):
            here = x_ref.at[chunk(i), pl.ds(0, PANEL)]
            z_copy(0, i, here, 1).start()
            z_copy(1, i, here, N - 1).start()
            mate_copy(i, here).start()

        p_ref[cc] = x_ref[:, :PANEL]

    relays = (zz != 0) & (zz != 4) & (zz != 5)

    @pl.when(zz != 0)
    def _():
        @pl.loop(0, CH)
        def _(i):
            here = p_ref.at[cc, chunk(i), :]
            z_copy(0, i, here, zz + step).wait_recv()

            @pl.when(relays)
            def _():
                z_copy(0, i, here, zz + step).start()

            mate_copy(i, here).start()

    @pl.loop(0, CH)
    def _(i):
        here = p_ref.at[1 - cc, chunk(i), :]
        remote(here, here, cs.at[i], cr.at[i], mate).wait_recv()

    x = x_ref[...]

    @pl.loop(0, 4)
    def _(b):
        block = p_ref[b // 2, :, pl.ds(pl.multiple_of(128 * lax.rem(b, 2), 128), 128)]
        terms = tdot(block, x)
        for k in range(2):
            for j in range(2):
                own[k, 2 * b + j, 0:PIECE, :] = terms[PIECE * j : PIECE * (j + 1), PANEL * k : PANEL * (k + 1)]

    gb = col // 4
    block = p_ref[gb // 2, :, pl.ds(pl.multiple_of(128 * lax.rem(gb, 2), 128), 128)]
    for k in range(2):
        gtmp[k] = tdot(block, p_ref[k])
    for k in range(2):
        for j in range(N):
            first = pl.multiple_of(32 * lax.rem(col, 4) + 8 * (j // 2), 8)
            own[k, j, PIECE : PIECE + 8, 0:128] = gtmp[k, pl.ds(first, 8), 128 * (j % 2) : 128 * (j % 2) + 128]
            own[k, j, PIECE : PIECE + 8, 128:PANEL] = jnp.zeros((8, PANEL - 128), F32)

    def copy1(k, o, slot):
        peer = wrap(main[k] + o)
        return remote(own.at[k, peer], r1.at[k, slot], s1.at[k, o - 1], q1.at[k, slot], at_main(k, peer))

    def copy2(k, o, slot):
        peer = wrap(other[k] + o)
        return remote(stage.at[k, peer], r2.at[k, slot], s2.at[k, o - 1], q2.at[k, slot], at_other(k, peer))

    for o in PEERS:
        for k in range(2):
            copy1(k, o, main[k]).start()
    for k in range(2):
        r1[k, main[k]] = own[k, main[k]]
        for o in PEERS:
            copy1(k, o, wrap(main[k] + o)).wait_recv()
        total = r1[k, 0]
        for o in range(1, N):
            total = total + r1[k, o]
        for i in range(N):
            stage[k, i, 0:8, :] = total[8 * i : 8 * i + 8, :]
            stage[k, i, 8:16, :] = total[PIECE : PIECE + 8, :]
        for o in PEERS:
            copy2(k, o, other[k]).start()
        r2[k, other[k]] = stage[k, other[k]]

    def rows_of(k, i):
        return cf.at[k, pl.ds(pl.multiple_of(PIECE * main[k] + 8 * i, 8), 8), :]

    def piece_of(k, i):
        return cf.at[k, pl.ds(pl.multiple_of(PIECE * i, PIECE), PIECE), :]

    def copy3(k, o, i):
        return remote(rows_of(k, i), rows_of(k, i), s3.at[k, o - 1], q3.at[k, i], at_other(k, wrap(other[k] + o)))

    def copy4(k, o, i):
        return remote(piece_of(k, i), piece_of(k, i), s4.at[k, o - 1], q4.at[k, i], at_main(k, wrap(main[k] + o)))

    def tile_copy(k, o, i):
        tile = gall.at[col, k, i]
        return remote(tile, tile, sg.at[k, o - 1], qg.at[k, i], at_main(k, wrap(main[k] + o)))

    def slab_copy(o, z):
        slab = gall.at[z * 2 + cc]
        return remote(slab, slab, sz.at[o - 1], qz.at[z], at_z(zz + o))

    def slab_mate(z, core):
        slab = gall.at[z * 2 + core]
        return remote(slab, slab, sc.at[z], qc.at[z], mate)

    for k in range(2):
        for o in PEERS:
            copy2(k, o, wrap(other[k] + o)).wait_recv()
        total = r2[k, 0]
        for o in range(1, N):
            total = total + r2[k, o]
        gall[col, k, main[k]] = total[8:16, 0:128]
        cf[k, pl.ds(pl.multiple_of(PIECE * main[k] + 8 * other[k], 8), 8), :] = total[0:8, :]
        for o in PEERS:
            tile_copy(k, o, main[k]).start()
        for o in PEERS:
            copy3(k, o, other[k]).start()

    for k in range(2):
        for o in PEERS:
            tile_copy(k, o, wrap(main[k] + o)).wait_recv()
    for o in PEERS:
        slab_copy(o, zz).start()
    slab_mate(zz, cc).start()

    for k in range(2):
        for o in PEERS:
            copy3(k, o, wrap(other[k] + o)).wait_recv()
        for o in PEERS:
            copy4(k, o, main[k]).start()
    for o in PEERS:
        z = wrap(zz - o)
        slab_copy(o, z).wait_recv()
        slab_mate(z, cc).start()
    for k in range(2):
        for o in PEERS:
            copy4(k, o, wrap(main[k] + o)).wait_recv()
    for z in range(N):
        slab_mate(z, 1 - cc).wait_recv()

    @pl.loop(0, CH)
    def _(i):
        here = p_ref.at[cc, chunk(i), :]
        mate_copy(i, here).wait_send()

        @pl.when(relays | (zz == 0))
        def _():
            z_copy(0, i, here, zz + step).wait_send()

        @pl.when(zz == 0)
        def _():
            z_copy(1, i, here, N - 1).wait_send()

    for o in range(1, N):
        for k in range(2):
            copy1(k, o, main[k]).wait_send()
            copy2(k, o, other[k]).wait_send()
            copy3(k, o, other[k]).wait_send()
            copy4(k, o, main[k]).wait_send()
            tile_copy(k, o, main[k]).wait_send()
        slab_copy(o, zz).wait_send()
    for z in range(N):
        slab_mate(z, cc).wait_send()


def reduced(matrix):
    dma = pltpu.SemaphoreType.DMA
    out = lambda *shape: jax.ShapeDtypeStruct(shape, F32)
    vmem = pl.BlockSpec(memory_space=pltpu.VMEM)
    return pl.pallas_call(
        reduce_kernel,
        out_shape=(out(2, 512, PANEL), out(2, 512, PANEL), out(16, 2, N, 8, 128)),
        in_specs=[vmem],
        out_specs=(vmem, vmem, vmem),
        scratch_shapes=[
            pltpu.VMEM((2, N, 72, PANEL), F32),
            pltpu.VMEM((2, N, 72, PANEL), F32),
            pltpu.VMEM((2, N, 16, PANEL), F32),
            pltpu.VMEM((2, N, 16, PANEL), F32),
            pltpu.VMEM((2, 128, PANEL), F32),
            dma((2, CH)), dma((CH,)), dma((CH,)), dma((CH,)),
            *[dma((2, N))] * 8,
            dma((2, N)), dma((2, N)), dma((N,)), dma((N,)), dma((N,)), dma((N,)),
        ],
        compiler_params=pltpu.CompilerParams(collective_id=0, has_side_effects=True),
    )(matrix)


def solve_kernel(stretch, x_hbm, p_hbm, cf_hbm, gall, upd, w_hbm, g, m, t, e, bt, dcol, drow, x_ref, p_ref, cf, w_ref, sems):
    n = 2 * PANEL
    col = lax.axis_index("col")
    get_x = pltpu.make_async_copy(x_hbm, x_ref, sems.at[0])
    get_p = pltpu.make_async_copy(p_hbm, p_ref, sems.at[1])
    get_c = pltpu.make_async_copy(cf_hbm, cf, sems.at[2])
    put_w = pltpu.make_async_copy(w_ref, w_hbm, sems.at[3])
    get_c.start()
    get_p.start()
    get_x.start()

    @pl.loop(0, 16)
    def _(c):
        for k in range(2):
            for j in range(N):
                rows = pl.ds(pl.multiple_of(32 * c + 8 * (j // 2), 8), 8)
                g[rows, PANEL * k + 128 * (j % 2) : PANEL * k + 128 * (j % 2) + 128] = gall[c, k, j]

    i_row = lax.broadcasted_iota(jnp.int32, (n, n), 0)
    i_col = lax.broadcasted_iota(jnp.int32, (n, n), 1)
    eye = i_row == i_col
    diagonal = jnp.where(eye, g[...], 0.0)
    dcol[...] = lax.rsqrt(jnp.sum(diagonal, axis=1, keepdims=True))
    drow[...] = lax.rsqrt(jnp.sum(diagonal, axis=0, keepdims=True))
    g[...] = g[...] * dcol[...] * drow[...]

    ident = jnp.where(eye, 1.0, 0.0)
    b_row = lax.broadcasted_iota(jnp.int32, (PANEL, PANEL), 0)
    b_col = lax.broadcasted_iota(jnp.int32, (PANEL, PANEL), 1)
    b_eye = jnp.where(b_row == b_col, 1.0, 0.0)

    def half_lower(v):
        return jnp.where(b_row > b_col, v, 0.5 * b_eye * v)

    halves = [pl.ds(0, PANEL), pl.ds(PANEL, PANEL)]
    top, low = halves
    m[top, top] = b_eye - half_lower(g[top, top] - b_eye)
    m[low, low] = b_eye - half_lower(g[low, low] - b_eye)
    m[low, top] = -g[low, top]
    m[top, low] = jnp.zeros((PANEL, PANEL), F32)

    def refine(precision):
        t[top, top] = dot(m[top, top], g[top, top], precision)
        for h in halves:
            t[low, h] = dot(m[low, top], g[top, h], precision) + dot(m[low, low], g[low, h], precision)
        e00 = dott(t[top, top], m[top, top], precision) - b_eye
        e10 = dott(t[low, top], m[top, top], precision)
        e11 = dott(t[low, top], m[low, top], precision) + dott(t[low, low], m[low, low], precision) - b_eye
        square = jnp.sum(e00 * e00 + 2.0 * e10 * e10 + e11 * e11)
        e[top, top] = half_lower(e00)
        e[low, top] = e10
        e[low, low] = half_lower(e11)
        below = dot(e[low, top], m[top, top], precision) + dot(e[low, low], m[low, top], precision)
        m[low, top] = m[low, top] - below
        m[top, top] = m[top, top] - dot(e[top, top], m[top, top], precision)
        m[low, low] = m[low, low] - dot(e[low, low], m[low, low], precision)
        return square

    refine(lax.Precision.DEFAULT)
    refine(lax.Precision.HIGH)
    left = refine(HI)

    @pl.when(jnp.logical_not(left < 1e-6))
    def _():
        t[...] = ident

        @pl.loop(0, n)
        def _(j):
            g_row = g[pl.ds(j, 1), :]
            t_row = t[pl.ds(j, 1), :]
            lane = lax.broadcasted_iota(jnp.int32, (n, n), 1)
            column = jnp.sum(jnp.where(lane == j, g[...], 0.0), axis=1, keepdims=True)
            one_lane = lax.broadcasted_iota(jnp.int32, (1, n), 1)
            pivot = jnp.sum(jnp.where(one_lane == j, g_row, 0.0), axis=1, keepdims=True)
            down = lax.broadcasted_iota(jnp.int32, (n, 1), 0)
            factor = jnp.where(down > j, column / pivot, 0.0)
            scale = jnp.where(down == j, lax.rsqrt(pivot), 1.0)
            g[...] = g[...] - factor * g_row
            t[...] = (t[...] - factor * t_row) * scale

        m[...] = t[...]

    m[...] = m[...] * drow[...]
    get_c.wait()
    for k, h in enumerate(halves):
        c_top, c_low = cf[k, top, :], cf[k, low, :]
        w_ref[top, h] = dot(m[top, top], c_top)
        w_ref[low, h] = dot(m[low, top], c_top) + dot(m[low, low], c_low)
    put_w.start()
    get_p.wait()
    get_x.wait()
    bt[:, top] = dott(p_ref[0], m[top, top])
    bt[:, low] = dott(p_ref[0], m[low, top]) + dott(p_ref[1], m[low, low])
    upd[:, low] = x_ref[:, low] - dot(bt[...], w_ref[:, low])
    first = x_ref[:, top] - dot(bt[:, top], w_ref[top, top])
    first = jnp.where(col == 0, stretch * bt[:, top], first)
    first = first - dot(bt[:, low], w_ref[low, top])
    upd[:, top] = jnp.where(col == 1, stretch * bt[:, low], first)
    put_w.wait()


def solved(stretch, matrix, panels, cross, gram):
    vmem = pl.BlockSpec(memory_space=pltpu.VMEM)
    anywhere = pl.BlockSpec(memory_space=pl.ANY)
    square = pltpu.VMEM((512, 512), F32)
    return pl.pallas_call(
        functools.partial(solve_kernel, stretch),
        out_shape=(jax.ShapeDtypeStruct((512, 512), F32), jax.ShapeDtypeStruct((512, 512), F32)),
        in_specs=[anywhere] * 3 + [vmem],
        out_specs=(vmem, anywhere),
        scratch_shapes=[square] * 5
        + [pltpu.VMEM((512, 1), F32), pltpu.VMEM((1, 512), F32), square]
        + [pltpu.VMEM((2, 512, PANEL), F32)] * 2
        + [square, pltpu.SemaphoreType.DMA((4,))],
    )(matrix, panels, cross, gram)


def body(matrix):
    stretch = math.sqrt(lax.axis_size("row") * matrix.shape[0])
    panels, cross, gram = reduced(matrix)
    return solved(stretch, matrix, panels, cross, gram)


def solution(mesh):
    in_specs = (P("row", "col"),)
    out_specs = (P("row", "col"), P(None, "col"))
    return jax.shard_map(body, mesh=mesh, in_specs=in_specs, out_specs=out_specs, check_vma=False)
```
